32 devices in a mesh: dp: 2 (over x), tensor: 4 (over y, core), latent: 4 (over z).
Axes of the slice: x: 2, y: 2, z: 4, core: 2. Of those that a mesh axis runs over, the one named last changes fastest.
Arguments:
- residual: bfloat16 [256, 4608], P('dp', ('tensor', 'latent')), may hold values from -6 to 6
- segments: int32 [2, 128], P('dp'), may hold values from 0 to 3, never falling along the last dimension, each value on 1 to 64 neighbouring positions
- row_perm: int32 [256], P('dp'), may hold values from 0 to 255, as said below
- pre_gain: float32 [4608], replicated, may hold values from 0.25 to 1.75
- post_gain: float32 [4608], replicated, may hold values from 0.25 to 1.75
- w_query: bfloat16 [4608, 4096], P(None, ('tensor', 'latent')), may hold values from -0.70710678 to 0.70710678
- w_key: bfloat16 [4608, 2048], P(None, ('tensor', 'latent')), may hold values from -0.09375 to 0.09375
- w_value: bfloat16 [4608, 2048], P(None, ('tensor', 'latent')), may hold values from -0.09375 to 0.09375
- w_out: bfloat16 [4096, 4608], P(('tensor', 'latent')), may hold values from -0.09375 to 0.09375
- sae_weight: bfloat16 [4608, 16384], P('dp', ('tensor', 'latent')), may hold values from -0.09375 to 0.09375
- enc_bias: float32 [16384], P(('tensor', 'latent')), may hold values from -3 to 3
- thresholds: float32 [16384], P(('tensor', 'latent')), may hold values from 0.2 to 1.2
- dec_bias: float32 [4608], replicated, may hold values from -3 to 3
Outputs:
- weight_grad: bfloat16 [4608, 16384], P('dp', ('tensor', 'latent'))
- bias_grad: float32 [16384], P(('tensor', 'latent'))
- codes: bfloat16 [256, 16384], P('dp', ('tensor', 'latent'))
The draws below stay inside these ranges and needn't reach their ends.
Inputs may be any that keep to these rules, and one draw needn't show every extreme that they name: `segments`: segment numbers never fall along a row. row_perm is a permutation. Within the rows 128 g to 128 (g + 1) - 1, the 64 rows starting at 128 g + s * 64 hold only indices from 128 s to 128 (s + 1) - 1.
All inputs are finite; a program needn't handle non-finite values.
Results may differ from the reference program's by a relative error of at most 0.03.
Values may be sent and summed in bfloat16 or wider, within the bound.
No kernel may reach another device: no remote copies, remote signals or barrier semaphores. Data moves between devices by JAX's collectives and lax.ppermute only.
A program may use at most 128 MiB of HBM per device.

```python
import math
import jax
import jax.numpy as jnp
import numpy as np
from jax import lax

D = 4608
HEADS = 32
KV_HEADS = 16
HEAD = 128
LATENTS = 16384
TOK_G = 128
GROUPS = 2
TOKENS = 256
BLOCK = 64


def draw_row_perm(key, part):
    keys = jax.random.split(key, GROUPS)
    orders = jax.vmap(lambda single_key: jax.random.permutation(single_key, TOK_G))(keys)
    orders = orders.astype(jnp.int32).reshape(GROUPS, GROUPS, BLOCK)
    orders = orders + (jnp.arange(GROUPS, dtype=jnp.int32) * TOK_G)[:, None, None]
    return jnp.transpose(orders, (1, 0, 2)).reshape(TOKENS).astype(jnp.int32)


def draw_w_query(key, part):
    head_key, entry_key = jax.random.split(jax.random.fold_in(key, 11))
    head_scale = jnp.exp(jax.random.uniform(head_key, (HEADS,), jnp.float32, 0.0, math.log(12.0)))
    entries = jnp.clip(jax.random.normal(entry_key, (D, HEADS, HEAD), jnp.float32), -4.0, 4.0)
    weight = entries * head_scale[None, :, None] * D ** (-0.5)
    return weight.reshape(D, HEADS * HEAD).astype(jnp.bfloat16)


def level_of(stream_key, shape, shards, least, largest):
    level = 1.0
    for dim, parts in shards:
        steps = jax.random.uniform(jax.random.fold_in(jax.random.fold_in(stream_key, 6), dim), (parts,), jnp.float32, least / len(shards), largest / len(shards))
        level = level * jnp.repeat(jnp.exp(steps), shape[dim] // parts).reshape((-1,) + (1,) * (len(shape) - 1 - dim))
    return level


def length_profile(number_of, total, limit, lean):
    portions = [(1 << 20) // math.isqrt(rank ** lean) + 1 for rank in range(2, number_of + 1)]
    rest, holding = total - limit - (number_of - 1), [1] * (number_of - 1)
    while rest > 0:
        movable = [i for i in range(number_of - 1) if holding[i] < limit]
        pool, left = sum([portions[i] for i in movable]), rest
        for i in movable:
            extra = min(limit - holding[i], max(1, left * portions[i] // pool), rest)
            holding[i] = holding[i] + extra
            rest = rest - extra
    return np.array([limit] + holding)


def ragged_sizes(rng, amount, total, reach, skew):
    if amount == 2:
        one = jax.random.randint(rng, (), max(1, total - reach), min(reach, total - 1) + 1)
        return jnp.stack([one, total - one])
    sizes = jnp.asarray(length_profile(amount, total, reach, skew), jnp.int32)
    twos = (amount - 1) // 2
    source_of, sink = sizes[1:1 + 2 * twos:2], sizes[2:2 + 2 * twos:2]
    margin = jnp.minimum(source_of - 1, reach - sink)
    moved = jax.random.randint(jax.random.fold_in(rng, 1), (twos,), 0, 1 << 20) % (margin + 1)
    sizes = sizes.at[1:1 + 2 * twos:2].set(source_of - moved).at[2:2 + 2 * twos:2].set(sink + moved)
    return sizes[jax.random.permutation(jax.random.fold_in(rng, 2), amount)]


def centred(own_key, dims, deviation, reach, cuts=(), kind=jnp.bfloat16):
    values = deviation * jax.random.normal(own_key, dims, jnp.float32)
    if cuts:
        values = values * level_of(own_key, dims, cuts, -0.22, 0.18)
    return jnp.clip(values, -reach, reach).astype(kind)


def setup_inputs(seed: int = 0) -> dict:
    arg_keys = jax.random.split(jax.random.key(seed), 14)
    return {
        "residual": centred(arg_keys[0], (TOKENS, D), 1.0, 6.0, ((0, 2), (1, 16))),
        "segments": jax.vmap(lambda own: jnp.searchsorted(jnp.cumsum(ragged_sizes(own, 4, TOK_G, TOK_G // 2, 0)), jnp.arange(TOK_G), side="right"))(jax.random.split(arg_keys[1], GROUPS)).reshape((GROUPS, TOK_G)).astype(jnp.int32),
        "row_perm": draw_row_perm(jax.random.fold_in(arg_keys[13], 71), 0),
        "pre_gain": jnp.clip(1.0 + 0.15 * jax.random.normal(arg_keys[3], (D,), jnp.float32), 0.25, 1.75),
        "post_gain": jnp.clip(1.0 + 0.15 * jax.random.normal(arg_keys[4], (D,), jnp.float32), 0.25, 1.75),
        "w_query": draw_w_query(jax.random.fold_in(arg_keys[13], 71), 0),
        "w_key": centred(arg_keys[6], (D, KV_HEADS * HEAD), D ** -0.5, 0.09375, ((1, 16),)),
        "w_value": centred(arg_keys[7], (D, KV_HEADS * HEAD), D ** -0.5, 0.09375, ((1, 16),)),
        "w_out": centred(arg_keys[8], (HEADS * HEAD, D), (HEADS * HEAD) ** -0.5, 0.09375, ((0, 16),)),
        "sae_weight": centred(arg_keys[9], (D, LATENTS), D ** -0.5, 0.09375, ((0, 2), (1, 16))),
        "enc_bias": centred(arg_keys[10], (LATENTS,), 0.5, 3.0, ((0, 16),), jnp.float32),
        "thresholds": jnp.clip(0.2 + 1 * jax.random.uniform(arg_keys[11], (LATENTS,), jnp.float32) ** level_of(arg_keys[11], (LATENTS,), ((0, 16),), -0.2, 0.2), 0.2, 1.2),
        "dec_bias": centred(arg_keys[12], (D,), 0.5, 3.0, (), jnp.float32),
    }


epsilon = 1e-06
softcap = 50.0
ramp_width = 0.05
rotary_base = 10000.0

def rms_scale(field, gain_vec):
    return field * lax.rsqrt(lax.optimization_barrier(jnp.mean(field * field, axis=-1, keepdims=True)) + epsilon) * gain_vec

def rotate(field, positions):
    half_width = field.shape[-1] // 2
    frequency = rotary_base ** (-2.0 * jnp.arange(half_width, dtype=jnp.float32) / field.shape[-1])
    angles = positions[..., :, None, None] * frequency
    cosine = jnp.cos(angles)
    sine_part = jnp.sin(angles)
    first_half = field[..., :half_width]
    second_half = field[..., half_width:]
    return jnp.concatenate([first_half * cosine - second_half * sine_part, second_half * cosine + first_half * sine_part], axis=-1)

def doc_masks(segment_ids):
    same_doc = segment_ids[..., :, None] == segment_ids[..., None, :]
    indices = jnp.arange(segment_ids.shape[-1], dtype=jnp.int32)
    earlier = indices[None, :] < indices[:, None]
    positions = lax.optimization_barrier(jnp.sum((same_doc & earlier).astype(jnp.float32), axis=-1))
    attend_mask = (same_doc & (indices[None, :] <= indices[:, None])).astype(jnp.float32)
    return (positions, attend_mask)

def reference(residual, segments, row_perm, pre_gain, post_gain, w_query, w_key, w_value, w_out, sae_weight, enc_bias, thresholds, dec_bias):
    stream = residual.astype(jnp.float32)
    normed = rms_scale(stream, pre_gain).astype(jnp.bfloat16)
    positions, attend_mask = doc_masks(segments)
    group_ratio = HEADS // KV_HEADS
    query_projected = jnp.dot(normed, w_query, preferred_element_type=jnp.float32).reshape(GROUPS, TOK_G, HEADS, HEAD)
    query_projected = rotate(query_projected, positions).astype(jnp.bfloat16).reshape(GROUPS, TOK_G, KV_HEADS, group_ratio, HEAD)
    key_projected = jnp.dot(normed, w_key, preferred_element_type=jnp.float32).reshape(GROUPS, TOK_G, KV_HEADS, HEAD)
    key_projected = rotate(key_projected, positions).astype(jnp.bfloat16)
    value_projected = jnp.dot(normed, w_value, preferred_element_type=jnp.float32).astype(jnp.bfloat16).reshape(GROUPS, TOK_G, KV_HEADS, HEAD)
    logit_matrix = jnp.einsum('btgrd,bsgd->bgrts', query_projected.astype(jnp.float32), key_projected.astype(jnp.float32)) * (D / HEADS) ** (-0.5)
    logit_matrix = softcap * jnp.tanh(logit_matrix / softcap)
    weighted = jnp.exp(logit_matrix) * attend_mask[:, None, None]
    attention_weights = (weighted / lax.optimization_barrier(jnp.sum(weighted, axis=-1, keepdims=True))).astype(jnp.bfloat16)
    head_out = jnp.einsum('bgrts,bsgd->btgrd', attention_weights.astype(jnp.float32), value_projected.astype(jnp.float32))
    head_out = head_out.astype(jnp.bfloat16).reshape(TOKENS, HEADS * HEAD)
    attn_out = jnp.dot(head_out, w_out, preferred_element_type=jnp.float32)
    hidden = (stream + rms_scale(attn_out, post_gain)).astype(jnp.bfloat16)
    sae_rows = hidden[row_perm]
    pre_acts = jnp.dot(sae_rows, sae_weight, preferred_element_type=jnp.float32) + enc_bias
    open_gate = jax.nn.sigmoid((pre_acts - thresholds) / ramp_width)
    latent_acts = (pre_acts * open_gate).astype(jnp.bfloat16)
    contract_last = (((1,), (1,)), ((), ()))
    rebuilt = lax.dot_general(latent_acts, sae_weight, contract_last, preferred_element_type=jnp.float32)
    error_bf = (rebuilt + dec_bias - sae_rows.astype(jnp.float32)).astype(jnp.bfloat16)
    latent_gradient = jnp.dot(error_bf, sae_weight, preferred_element_type=jnp.float32)
    slope = open_gate + pre_acts * open_gate * (1.0 - open_gate) / ramp_width
    grad_pre = (latent_gradient * slope).astype(jnp.bfloat16)
    grad_scale = TOKENS ** (-0.5)
    contract_first = (((0,), (0,)), ((), ()))

    def add_group(running, group_items):
        rows_part, error_part, grad_part, acts_part = group_items
        group_term = lax.dot_general(rows_part, grad_part, contract_first, preferred_element_type=jnp.float32)
        group_term = group_term + lax.dot_general(error_part, acts_part, contract_first, preferred_element_type=jnp.float32)
        rounded = lax.optimization_barrier((grad_scale * group_term).astype(jnp.bfloat16))
        return (running + rounded.astype(jnp.float32), None)
    group_items = (sae_rows.reshape(GROUPS, TOK_G, D), error_bf.reshape(GROUPS, TOK_G, D), grad_pre.reshape(GROUPS, TOK_G, LATENTS), latent_acts.reshape(GROUPS, TOK_G, LATENTS))
    running, _ = lax.scan(add_group, jnp.zeros((D, LATENTS), jnp.float32), group_items)
    weight_grad = running.astype(jnp.bfloat16)
    bias_grad = grad_scale * lax.optimization_barrier(jnp.sum(grad_pre.astype(jnp.float32), axis=0))
    return (weight_grad, bias_grad, latent_acts)
```

```python
import math

import jax
import jax.numpy as jnp
from jax import lax
from jax.sharding import PartitionSpec as P

D = 4608
HEADS = 32
HEAD = 128

epsilon = 1e-06
softcap = 50.0
ramp_width = 0.05
rotary_base = 10000.0
BF = jnp.bfloat16
F32 = jnp.float32


def swap(values, axis, mask):
    size = lax.axis_size(axis)
    return lax.ppermute(values, axis, [(i, i ^ mask) for i in range(size)])


def plane_stages():
    tensor, latent = lax.axis_size("tensor"), lax.axis_size("latent")
    cores = 2 if tensor % 2 == 0 else 1
    stages = []
    if cores > 1:
        stages.append(("tensor", [1]))
    if tensor > cores:
        stages.append(("tensor", [k * cores for k in range(1, tensor // cores)]))
    if latent > 1:
        stages.append(("latent", list(range(1, latent))))
    return stages


def plane_index():
    tensor, latent = lax.axis_size("tensor"), lax.axis_size("latent")
    cores = 2 if tensor % 2 == 0 else 1
    t, z = lax.axis_index("tensor"), lax.axis_index("latent")
    return ((t % cores) * (tensor // cores) + t // cores) * latent + z


def gather_blocks(block):
    for axis, masks in reversed(plane_stages()):
        block = jnp.concatenate([block] + [swap(block, axis, m) for m in masks], axis=0)
    return block


def scatter_sum(partial):
    for axis, masks in plane_stages():
        parts = partial.reshape((len(masks) + 1, -1) + partial.shape[1:])
        total = parts[0].astype(F32)
        for place, m in enumerate(masks):
            total = total + swap(parts[place + 1].astype(BF), axis, m).astype(F32)
        partial = total
    return partial


def rotate(field, positions):
    half_width = field.shape[-1] // 2
    frequency = rotary_base ** (-2.0 * jnp.arange(half_width, dtype=F32) / field.shape[-1])
    angles = positions[..., :, None, None] * frequency
    cosine = jnp.cos(angles)
    sine_part = jnp.sin(angles)
    first_half = field[..., :half_width]
    second_half = field[..., half_width:]
    return jnp.concatenate(
        [
            first_half * cosine - second_half * sine_part,
            second_half * cosine + first_half * sine_part,
        ],
        axis=-1,
    )


def doc_masks(segment_ids):
    same_doc = segment_ids[..., :, None] == segment_ids[..., None, :]
    indices = jnp.arange(segment_ids.shape[-1], dtype=jnp.int32)
    earlier = indices[None, :] < indices[:, None]
    positions = jnp.sum((same_doc & earlier).astype(F32), axis=-1)
    attend_mask = (same_doc & (indices[None, :] <= indices[:, None])).astype(F32)
    return (positions, attend_mask)


def attention(stream_t, segments, pre_gain, w_query, w_key, w_value):
    length = stream_t.shape[1]
    stream = stream_t.astype(F32)
    normed_t = (
        stream
        * lax.rsqrt(jnp.mean(stream * stream, axis=0, keepdims=True) + epsilon)
        * pre_gain[:, None]
    ).astype(BF)
    positions, attend_mask = doc_masks(segments)
    query_heads = w_query.shape[1] // HEAD
    key_heads = w_key.shape[1] // HEAD
    ratio = query_heads // key_heads
    first = (((0,), (0,)), ((), ()))

    def project(weight):
        return lax.dot_general(normed_t, weight, first, preferred_element_type=F32).reshape(
            length, -1, HEAD
        )

    query = rotate(project(w_query), positions).astype(BF)
    query = query.reshape(length, key_heads, ratio, HEAD)
    key = rotate(project(w_key), positions).astype(BF)
    value = project(w_value).astype(BF)
    logits = jnp.einsum("zjei,kji->jezk", query, key, preferred_element_type=F32)
    logits = logits * (D / HEADS) ** (-0.5)
    logits = softcap * jnp.tanh(logits / softcap)
    weighted = jnp.exp(logits) * attend_mask
    probs = (weighted / jnp.sum(weighted, axis=-1, keepdims=True)).astype(BF)
    head_out = jnp.einsum("jzku,ujw->kjzw", probs, value, preferred_element_type=F32)
    return head_out.astype(BF).reshape(length, query_heads * HEAD)


def local(
    residual,
    segments,
    row_perm,
    pre_gain,
    post_gain,
    w_query,
    w_key,
    w_value,
    w_out,
    sae_weight,
    enc_bias,
    thresholds,
    dec_bias,
):
    groups = lax.axis_size("dp")
    tensor, latent = lax.axis_size("tensor"), lax.axis_size("latent")
    plane = tensor * latent
    length = residual.shape[0]
    rows = length // plane
    half = sae_weight.shape[0]
    me = plane_index()
    mine = lax.axis_index("dp")
    cores = 2 if tensor % 2 == 0 else 1
    contract_last = (((1,), (1,)), ((), ()))
    contract_first = (((0,), (0,)), ((), ()))

    blocks = gather_blocks(residual.T[None])
    flat = jnp.arange(plane, dtype=jnp.int32)
    t_of, z_of = flat // latent, flat % latent
    number = ((t_of % cores) * (tensor // cores) + t_of // cores) * latent + z_of
    stream_t = blocks[number ^ me].reshape(-1, length)

    head_out = attention(stream_t, segments[0], pre_gain, w_query, w_key, w_value)
    head_out = head_out.reshape(plane, rows, -1)[flat ^ me].reshape(length, -1)
    partial = jnp.dot(head_out, w_out, preferred_element_type=F32)
    attn_out = scatter_sum(partial)
    own = lax.dynamic_slice(stream_t, (0, me * rows), (stream_t.shape[0], rows)).T.astype(F32)
    scale = lax.rsqrt(jnp.mean(attn_out * attn_out, axis=-1, keepdims=True) + epsilon)
    hidden = (own + attn_out * scale * post_gain).astype(BF)
    pieces = hidden.reshape(rows, groups, half).transpose(1, 0, 2)

    def piece(k):
        return lax.dynamic_index_in_dim(pieces, mine ^ k, 0, keepdims=False)

    kept = gather_blocks(piece(0))
    others = jnp.stack([swap(piece(k), "dp", k) for k in range(1, groups)], 0)

    def spread(stack):
        count = stack.shape[0]
        flat_stack = stack.transpose(1, 0, 2).reshape(rows, count * half) if count > 1 else stack[0]
        out = gather_blocks(flat_stack)
        if count > 1:
            out = out.reshape(length, count, half).transpose(1, 0, 2)
            return out.reshape(count * length, half)
        return out

    sae = [kept, spread(others)]

    def across(first_part, rest):
        if groups == 2:
            got_rest = swap(first_part.astype(BF), "dp", 1).astype(F32)
            got_first = swap(rest.astype(BF), "dp", 1).astype(F32)
            return first_part + got_first, rest + got_rest
        total = jnp.concatenate([first_part, rest], 0)
        masks = [1 << k for k in range(groups.bit_length() - 1)]
        for m in reversed(masks):
            keep, send = jnp.split(total, 2, axis=0)
            total = keep + swap(send.astype(BF), "dp", m).astype(F32)
        for m in masks:
            total = jnp.concatenate([total, swap(total, "dp", m)], 0)
        return total[:length], total[length:]

    pre = across(*[jnp.dot(s, sae_weight, preferred_element_type=F32) for s in sae])
    pre = [p + enc_bias for p in pre]
    gates = [jax.nn.sigmoid((p - thresholds) / ramp_width) for p in pre]
    codes = [(p * g).astype(BF) for p, g in zip(pre, gates)]
    slopes = [g + p * g * (1.0 - g) / ramp_width for p, g in zip(pre, gates)]

    half_bias = lax.dynamic_slice(dec_bias, (mine * half,), (half,))

    def rebuild(chunk, count):
        part = lax.dot_general(codes[chunk], sae_weight, contract_last, preferred_element_type=F32)
        if count > 1:
            part = part.reshape(count, plane, rows, half).transpose(1, 0, 2, 3)
            part = part.reshape(plane * count * rows, half)
        total = scatter_sum(part)
        if count > 1:
            held = sae[chunk].reshape(count, plane, rows, half)[:, 0].reshape(count * rows, half)
        else:
            held = sae[chunk][:rows]
        error = (total + half_bias - held.astype(F32)).astype(BF)
        out = gather_blocks(error)
        if count > 1:
            out = out.reshape(plane, count, rows, half).transpose(1, 0, 2, 3)
            out = out.reshape(count * length, half)
        return out

    error = [None, None]
    error[1] = rebuild(1, groups - 1)
    error[0] = rebuild(0, 1)
    back = across(*[jnp.dot(e, sae_weight, preferred_element_type=F32) for e in error])
    grad_pre = [(b * s).astype(BF) for b, s in zip(back, slopes)]

    grad_scale = 1.0 / math.sqrt(length * groups)
    left = jnp.concatenate(sae + error, 0)
    all_codes = jnp.concatenate(codes, 0)
    all_grad = jnp.concatenate(grad_pre, 0)
    right = jnp.concatenate([all_grad, all_codes], 0)
    weight_grad = lax.dot_general(left, right, contract_first, preferred_element_type=F32)
    weight_grad = (grad_scale * weight_grad).astype(BF)
    bias_grad = grad_scale * jnp.sum(all_grad.astype(F32), axis=0)

    place = row_perm ^ ((mine * plane + me) * rows)
    chosen = (place[:, None] == jnp.arange(length * groups, dtype=jnp.int32)[None, :]).astype(BF)
    out_codes = jnp.dot(chosen, all_codes, preferred_element_type=F32).astype(BF)
    return (weight_grad, bias_grad, out_codes)


def solution(mesh):
    return jax.shard_map(
        local,
        mesh=mesh,
        in_specs=(
            P("dp", ("tensor", "latent")),
            P("dp", None),
            P("dp"),
            P(),
            P(),
            P(None, ("tensor", "latent")),
            P(None, ("tensor", "latent")),
            P(None, ("tensor", "latent")),
            P(("tensor", "latent"), None),
            P("dp", ("tensor", "latent")),
            P(("tensor", "latent")),
            P(("tensor", "latent")),
            P(),
        ),
        out_specs=(
            P("dp", ("tensor", "latent")),
            P(("tensor", "latent")),
            P("dp", ("tensor", "latent")),
        ),
        check_vma=False,
    )
```

```python
import math

import jax
import jax.numpy as jnp
from jax import lax
from jax.experimental import pallas as pl
from jax.experimental.pallas import tpu as pltpu
from jax.sharding import PartitionSpec as P

D = 4608
HEADS = 32
HEAD = 128

epsilon = 1e-06
softcap = 50.0
ramp_width = 0.05
rotary_base = 10000.0
BF = jnp.bfloat16
F32 = jnp.float32


def swap(values, axis, mask):
    size = lax.axis_size(axis)
    return lax.ppermute(values, axis, [(i, i ^ mask) for i in range(size)])


def plane_stages():
    tensor, latent = lax.axis_size("tensor"), lax.axis_size("latent")
    cores = 2 if tensor % 2 == 0 else 1
    stages = []
    if cores > 1:
        stages.append(("tensor", [1]))
    if tensor > cores:
        stages.append(("tensor", [k * cores for k in range(1, tensor // cores)]))
    if latent > 1:
        stages.append(("latent", list(range(1, latent))))
    return stages


def plane_index():
    tensor, latent = lax.axis_size("tensor"), lax.axis_size("latent")
    cores = 2 if tensor % 2 == 0 else 1
    t, z = lax.axis_index("tensor"), lax.axis_index("latent")
    return ((t % cores) * (tensor // cores) + t // cores) * latent + z


def gather_blocks(block):
    for axis, masks in reversed(plane_stages()):
        block = jnp.concatenate([block] + [swap(block, axis, m) for m in masks], axis=0)
    return block


def add_arrived(kept, sent, axis, masks):
    total = kept
    for m, part in zip(masks, sent):
        total = total + swap(part, axis, m).astype(F32)
    return total


def scatter_sum(partial, stages):
    for axis, masks in stages:
        parts = partial.reshape((len(masks) + 1, -1) + partial.shape[1:])
        sent = [parts[k + 1].astype(BF) for k in range(len(masks))]
        partial = add_arrived(parts[0].astype(F32), sent, axis, masks)
    return partial


def rotary_tables(positions):
    half_width = HEAD // 2
    frequency = rotary_base ** (-2.0 * jnp.arange(half_width, dtype=F32) / HEAD)
    angles = positions[:, None] * frequency
    cosine, sine = jnp.cos(angles), jnp.sin(angles)
    return jnp.concatenate([cosine, cosine], 1), jnp.concatenate([-sine, sine], 1)


def doc_masks(segment_ids):
    same_doc = segment_ids[..., :, None] == segment_ids[..., None, :]
    indices = jnp.arange(segment_ids.shape[-1], dtype=jnp.int32)
    earlier = indices[None, :] < indices[:, None]
    positions = jnp.sum((same_doc & earlier).astype(F32), axis=-1)
    attend_mask = (same_doc & (indices[None, :] <= indices[:, None])).astype(F32)
    return (positions, attend_mask)


def attention_body(
    sizes,
    feature_table,
    token_table,
    blocks,
    gain,
    cosine,
    sine,
    mask,
    pick,
    w_query,
    w_key,
    w_value,
    w_out,
    kept,
    sent,
    own,
    weight,
    weight_out,
    stream,
    normed,
    heads,
    sems,
):
    plane, columns, length, rows, query_heads, key_heads = sizes
    query_width, key_width = query_heads * HEAD, key_heads * HEAD
    starts = [0, query_width, query_width + key_width]
    copies = [
        pltpu.make_async_copy(src, weight.at[:, pl.ds(start, src.shape[1])], sems.at[k])
        for k, (src, start) in enumerate(zip((w_query, w_key, w_value), starts))
    ]
    copies.append(pltpu.make_async_copy(w_out, weight_out, sems.at[3]))
    for copy in copies:
        copy.start()
    squares = jnp.zeros((1, length), F32)
    for j in range(plane):
        block = blocks[feature_table[j]]
        stream[j * columns : (j + 1) * columns] = block
        wide = block.astype(F32)
        squares = squares + jnp.sum(wide * wide, axis=0, keepdims=True)
    scale = lax.rsqrt(squares / (plane * columns) + epsilon)
    for j in range(plane):
        part = slice(j * columns, (j + 1) * columns)
        normed[part] = (stream[part].astype(F32) * scale * gain[part]).astype(BF)
    own[...] = lax.dot_general(
        pick[...], stream[...], (((1,), (1,)), ((), ())), preferred_element_type=F32
    )
    for copy in copies[:3]:
        copy.wait()
    projected = lax.dot_general(
        normed[...], weight[...], (((0,), (0,)), ((), ())), preferred_element_type=F32
    )

    def turned(start):
        field = projected[:, start : start + HEAD]
        return (field * cosine[...] + pltpu.roll(field, HEAD // 2, 1) * sine[...]).astype(BF)

    for j in range(query_heads):
        group = j // (query_heads // key_heads)
        query = turned(j * HEAD)
        key = turned(starts[1] + group * HEAD)
        value = projected[:, starts[2] + group * HEAD : starts[2] + (group + 1) * HEAD].astype(BF)
        logits = lax.dot_general(
            query, key, (((1,), (1,)), ((), ())), preferred_element_type=F32
        ) * (D / HEADS) ** (-0.5)
        logits = softcap * jnp.tanh(logits / softcap)
        weighted = jnp.exp(logits) * mask[...]
        probs = (weighted / jnp.sum(weighted, axis=-1, keepdims=True)).astype(BF)
        heads[:, j * HEAD : (j + 1) * HEAD] = jnp.dot(probs, value, preferred_element_type=F32)
    moved = [heads[pl.ds(pl.multiple_of(token_table[k] * rows, 8), rows)] for k in range(plane)]
    moved = jnp.concatenate(moved, 0).astype(BF)
    copies[3].wait()
    middle = length // 2
    step = 512
    for start in range(0, weight_out.shape[1], step):
        part = slice(start, min(start + step, weight_out.shape[1]))
        product = jnp.dot(moved, weight_out[:, part], preferred_element_type=F32)
        kept[:, part] = product[:middle]
        sent[:, part] = product[middle:].astype(BF)


def attention(blocks, feature_table, token_table, segments, pre_gain, weights, me):
    plane, columns, length = blocks.shape
    rows = length // plane
    features = plane * columns
    w_query, w_key, w_value, w_out = weights
    sizes = (plane, columns, length, rows, w_query.shape[1] // HEAD, w_key.shape[1] // HEAD)
    positions, mask = doc_masks(segments)
    cosine, sine = rotary_tables(positions)
    gain = jnp.broadcast_to(pre_gain[:, None], (features, length))
    token = jnp.arange(length, dtype=jnp.int32)[None, :]
    pick = (token == me * rows + jnp.arange(rows, dtype=jnp.int32)[:, None]).astype(BF)
    vmem = pl.BlockSpec(memory_space=pltpu.VMEM)
    smem = pl.BlockSpec(memory_space=pltpu.SMEM)
    anywhere = pl.BlockSpec(memory_space=pl.ANY)
    width = w_query.shape[1] + w_key.shape[1] + w_value.shape[1]
    total = w_out.shape[1]
    return pl.pallas_call(
        lambda *refs: attention_body(sizes, *refs),
        out_shape=(
            jax.ShapeDtypeStruct((length // 2, total), F32),
            jax.ShapeDtypeStruct((length // 2, total), BF),
            jax.ShapeDtypeStruct((rows, features), F32),
        ),
        in_specs=[smem] * 2 + [vmem] * 6 + [anywhere] * 4,
        out_specs=(vmem,) * 3,
        scratch_shapes=[
            pltpu.VMEM((features, width), BF),
            pltpu.VMEM(w_out.shape, BF),
            pltpu.VMEM((features, length), BF),
            pltpu.VMEM((features, length), BF),
            pltpu.VMEM((length, w_query.shape[1]), F32),
            pltpu.SemaphoreType.DMA((4,)),
        ],
        cost_estimate=pl.CostEstimate(
            flops=2 * length * (features * width + w_query.shape[1] * total),
            bytes_accessed=2 * (features * width + w_out.size),
            transcendentals=0,
        ),
    )(
        feature_table,
        token_table,
        blocks,
        gain,
        cosine,
        sine,
        mask,
        pick,
        w_query,
        w_key,
        w_value,
        w_out,
    )


def local(
    residual,
    segments,
    row_perm,
    pre_gain,
    post_gain,
    w_query,
    w_key,
    w_value,
    w_out,
    sae_weight,
    enc_bias,
    thresholds,
    dec_bias,
):
    groups = lax.axis_size("dp")
    tensor, latent = lax.axis_size("tensor"), lax.axis_size("latent")
    plane = tensor * latent
    length = residual.shape[0]
    rows = length // plane
    half = sae_weight.shape[0]
    me = plane_index()
    mine = lax.axis_index("dp")
    cores = 2 if tensor % 2 == 0 else 1
    contract_last = (((1,), (1,)), ((), ()))
    contract_first = (((0,), (0,)), ((), ()))

    blocks = gather_blocks(residual.T[None])
    flat = jnp.arange(plane, dtype=jnp.int32)
    t_of, z_of = flat // latent, flat % latent
    number = ((t_of % cores) * (tensor // cores) + t_of // cores) * latent + z_of
    kept_rows, sent_rows, own = attention(
        blocks,
        number ^ me,
        flat ^ me,
        segments[0],
        pre_gain,
        (w_query, w_key, w_value, w_out),
        me,
    )
    stages = plane_stages()
    attn_out = scatter_sum(add_arrived(kept_rows, [sent_rows], *stages[0]), stages[1:])
    scale = lax.rsqrt(jnp.mean(attn_out * attn_out, axis=-1, keepdims=True) + epsilon)
    hidden = (own + attn_out * scale * post_gain).astype(BF)
    pieces = hidden.reshape(rows, groups, half).transpose(1, 0, 2)

    def piece(k):
        return lax.dynamic_index_in_dim(pieces, mine ^ k, 0, keepdims=False)

    kept = gather_blocks(piece(0))
    others = jnp.stack([swap(piece(k), "dp", k) for k in range(1, groups)], 0)

    def spread(stack):
        count = stack.shape[0]
        flat_stack = stack.transpose(1, 0, 2).reshape(rows, count * half) if count > 1 else stack[0]
        out = gather_blocks(flat_stack)
        if count > 1:
            out = out.reshape(length, count, half).transpose(1, 0, 2)
            return out.reshape(count * length, half)
        return out

    sae = [kept, spread(others)]

    def across(first_part, rest):
        if groups == 2:
            got_rest = swap(first_part.astype(BF), "dp", 1).astype(F32)
            got_first = swap(rest.astype(BF), "dp", 1).astype(F32)
            return first_part + got_first, rest + got_rest
        total = jnp.concatenate([first_part, rest], 0)
        masks = [1 << k for k in range(groups.bit_length() - 1)]
        for m in reversed(masks):
            keep, send = jnp.split(total, 2, axis=0)
            total = keep + swap(send.astype(BF), "dp", m).astype(F32)
        for m in masks:
            total = jnp.concatenate([total, swap(total, "dp", m)], 0)
        return total[:length], total[length:]

    pre = across(*[jnp.dot(s, sae_weight, preferred_element_type=F32) for s in sae])
    pre = [p + enc_bias for p in pre]
    gates = [jax.nn.sigmoid((p - thresholds) / ramp_width) for p in pre]
    codes = [(p * g).astype(BF) for p, g in zip(pre, gates)]
    slopes = [g + p * g * (1.0 - g) / ramp_width for p, g in zip(pre, gates)]

    half_bias = lax.dynamic_slice(dec_bias, (mine * half,), (half,))

    def rebuild(chunk, count):
        part = lax.dot_general(codes[chunk], sae_weight, contract_last, preferred_element_type=F32)
        if count > 1:
            part = part.reshape(count, plane, rows, half).transpose(1, 0, 2, 3)
            part = part.reshape(plane * count * rows, half)
        total = scatter_sum(part, stages)
        if count > 1:
            held = sae[chunk].reshape(count, plane, rows, half)[:, 0].reshape(count * rows, half)
        else:
            held = sae[chunk][:rows]
        error = (total + half_bias - held.astype(F32)).astype(BF)
        out = gather_blocks(error)
        if count > 1:
            out = out.reshape(plane, count, rows, half).transpose(1, 0, 2, 3)
            out = out.reshape(count * length, half)
        return out

    error = [None, None]
    error[1] = rebuild(1, groups - 1)
    error[0] = rebuild(0, 1)
    back = across(*[jnp.dot(e, sae_weight, preferred_element_type=F32) for e in error])
    grad_pre = [(b * s).astype(BF) for b, s in zip(back, slopes)]

    grad_scale = 1.0 / math.sqrt(length * groups)
    left = jnp.concatenate(lax.optimization_barrier(sae + error), 0)
    all_codes = jnp.concatenate(codes, 0)
    all_grad = jnp.concatenate(grad_pre, 0)
    right = jnp.concatenate([all_grad, all_codes], 0)
    weight_grad = lax.dot_general(left, right, contract_first, preferred_element_type=F32)
    weight_grad = (grad_scale * weight_grad).astype(BF)
    bias_grad = grad_scale * jnp.sum(all_grad.astype(F32), axis=0)

    place = row_perm ^ ((mine * plane + me) * rows)
    chosen = (place[:, None] == jnp.arange(length * groups, dtype=jnp.int32)[None, :]).astype(BF)
    out_codes = jnp.dot(chosen, all_codes, preferred_element_type=F32).astype(BF)
    return (weight_grad, bias_grad, out_codes)


def solution(mesh):
    return jax.shard_map(
        local,
        mesh=mesh,
        in_specs=(
            P("dp", ("tensor", "latent")),
            P("dp", None),
            P("dp"),
            P(),
            P(),
            P(None, ("tensor", "latent")),
            P(None, ("tensor", "latent")),
            P(None, ("tensor", "latent")),
            P(("tensor", "latent"), None),
            P("dp", ("tensor", "latent")),
            P(("tensor", "latent")),
            P(("tensor", "latent")),
            P(),
        ),
        out_specs=(
            P("dp", ("tensor", "latent")),
            P(("tensor", "latent")),
            P("dp", ("tensor", "latent")),
        ),
        check_vma=False,
    )
```

```python
import math

import jax
import jax.numpy as jnp
from jax import lax
from jax.experimental import pallas as pl
from jax.experimental.pallas import tpu as pltpu
from jax.sharding import PartitionSpec as P


D = 4608
HEADS = 32
HEAD = 128

epsilon = 1e-06
softcap = 50.0
ramp_width = 0.05
rotary_base = 10000.0
BF = jnp.bfloat16
F32 = jnp.float32
VMEM_LIMIT = 28 * 1024 * 1024


def swap(values, axis, mask):
    size = lax.axis_size(axis)
    return lax.ppermute(values, axis, [(i, i ^ mask) for i in range(size)])


def plane_stages():
    tensor, latent = lax.axis_size("tensor"), lax.axis_size("latent")
    cores = 2 if tensor % 2 == 0 else 1
    stages = []
    if cores > 1:
        stages.append(("tensor", [1]))
    if tensor > cores:
        stages.append(("tensor", [k * cores for k in range(1, tensor // cores)]))
    if latent > 1:
        stages.append(("latent", list(range(1, latent))))
    return stages


def plane_index():
    tensor, latent = lax.axis_size("tensor"), lax.axis_size("latent")
    cores = 2 if tensor % 2 == 0 else 1
    t, z = lax.axis_index("tensor"), lax.axis_index("latent")
    return ((t % cores) * (tensor // cores) + t // cores) * latent + z


def gather_blocks(block, gate=None):
    stages = plane_stages()
    for place in reversed(range(len(stages))):
        axis, masks = stages[place]
        pieces = [block] + [swap(block, axis, m) for m in masks]
        if place == 1 and gate is not None:
            pieces = gate(pieces)
        block = jnp.concatenate(pieces, axis=0)
    return block


def add_arrived(kept, sent, stage):
    axis, masks = stage
    total = kept
    for m, part in zip(masks, sent):
        total = total + swap(part, axis, m).astype(F32)
    return total


def scatter_sum(partial, done=0):
    for place, stage in enumerate(plane_stages()):
        if place < done:
            continue
        parts = partial.reshape((len(stage[1]) + 1, -1) + partial.shape[1:])
        sent = [parts[k + 1].astype(BF) for k in range(len(stage[1]))]
        partial = add_arrived(parts[0].astype(F32), sent, stage)
    return partial


def rotary_tables(positions):
    half_width = HEAD // 2
    frequency = rotary_base ** (-2.0 * jnp.arange(half_width, dtype=F32) / HEAD)
    angles = positions[:, None] * frequency
    cosine, sine = jnp.cos(angles), jnp.sin(angles)
    return jnp.concatenate([cosine, cosine], 1), jnp.concatenate([-sine, sine], 1)


def doc_masks(segment_ids):
    same_doc = segment_ids[..., :, None] == segment_ids[..., None, :]
    indices = jnp.arange(segment_ids.shape[-1], dtype=jnp.int32)
    earlier = indices[None, :] < indices[:, None]
    positions = jnp.sum((same_doc & earlier).astype(F32), axis=-1)
    attend_mask = (same_doc & (indices[None, :] <= indices[:, None])).astype(F32)
    return (positions, attend_mask)


def hold_on_chip(values, after):
    def body(source, _, held, sem):
        copy = pltpu.make_async_copy(source, held, sem)
        copy.start()
        copy.wait()

    return pl.pallas_call(
        body,
        out_shape=pltpu.VMEM(values.shape, values.dtype),
        in_specs=[pl.BlockSpec(memory_space=pltpu.HBM), pl.BlockSpec(memory_space=pl.ANY)],
        out_specs=pl.BlockSpec(memory_space=pltpu.VMEM),
        scratch_shapes=[pltpu.SemaphoreType.DMA],
        compiler_params=pltpu.CompilerParams(vmem_limit_bytes=1024 * 1024),
        cost_estimate=pl.CostEstimate(
            flops=0, bytes_accessed=2 * values.size, transcendentals=0
        ),
    )(values, after)


def attention_body(
    sizes,
    feature_table,
    token_table,
    blocks,
    gain,
    cosine,
    sine,
    mask,
    pick,
    w_query,
    w_key,
    w_value,
    w_out,
    kept,
    sent,
    own,
    weight,
    weight_out,
    stream,
    normed,
    heads,
    sems,
):
    plane, columns, length, rows, query_heads, key_heads = sizes
    query_width, key_width = query_heads * HEAD, key_heads * HEAD
    starts = [0, query_width, query_width + key_width]
    copies = [
        pltpu.make_async_copy(src, weight.at[:, pl.ds(start, src.shape[1])], sems.at[k])
        for k, (src, start) in enumerate(zip((w_query, w_key, w_value), starts))
    ]
    copies.append(pltpu.make_async_copy(w_out, weight_out, sems.at[3]))
    for copy in copies:
        copy.start()
    squares = jnp.zeros((1, length), F32)
    for j in range(plane):
        block = blocks[feature_table[j]]
        stream[j * columns : (j + 1) * columns] = block
        wide = block.astype(F32)
        squares = squares + jnp.sum(wide * wide, axis=0, keepdims=True)
    scale = lax.rsqrt(squares / (plane * columns) + epsilon)
    for j in range(plane):
        part = slice(j * columns, (j + 1) * columns)
        normed[part] = (stream[part].astype(F32) * scale * gain[part]).astype(BF)
    own[...] = lax.dot_general(
        pick[...], stream[...], (((1,), (1,)), ((), ())), preferred_element_type=F32
    )
    for copy in copies[:3]:
        copy.wait()
    projected = lax.dot_general(
        normed[...], weight[...], (((0,), (0,)), ((), ())), preferred_element_type=F32
    )

    def turned(start):
        field = projected[:, start : start + HEAD]
        return (field * cosine[...] + pltpu.roll(field, HEAD // 2, 1) * sine[...]).astype(BF)

    for j in range(query_heads):
        group = j // (query_heads // key_heads)
        query = turned(j * HEAD)
        key = turned(starts[1] + group * HEAD)
        value = projected[:, starts[2] + group * HEAD : starts[2] + (group + 1) * HEAD].astype(BF)
        logits = lax.dot_general(
            query, key, (((1,), (1,)), ((), ())), preferred_element_type=F32
        ) * (D / HEADS) ** (-0.5)
        logits = softcap * jnp.tanh(logits / softcap)
        weighted = jnp.exp(logits) * mask[...]
        probs = (weighted / jnp.sum(weighted, axis=-1, keepdims=True)).astype(BF)
        heads[:, j * HEAD : (j + 1) * HEAD] = jnp.dot(probs, value, preferred_element_type=F32)
    moved = [heads[pl.ds(pl.multiple_of(token_table[k] * rows, 8), rows)] for k in range(plane)]
    moved = jnp.concatenate(moved, 0).astype(BF)
    copies[3].wait()
    middle = length // 2
    step = 512
    for start in range(0, weight_out.shape[1], step):
        part = slice(start, min(start + step, weight_out.shape[1]))
        product = jnp.dot(moved, weight_out[:, part], preferred_element_type=F32)
        kept[:, part] = product[:middle]
        sent[:, part] = product[middle:].astype(BF)


def attention_tables(segments, pre_gain, me, rows):
    length = segments.shape[0]
    positions, mask = doc_masks(segments)
    cosine, sine = rotary_tables(positions)
    gain = jnp.broadcast_to(pre_gain[:, None], (pre_gain.shape[0], length))
    token = jnp.arange(length, dtype=jnp.int32)[None, :]
    pick = (token == me * rows + jnp.arange(rows, dtype=jnp.int32)[:, None]).astype(BF)
    return gain, cosine, sine, mask, pick


def attention(blocks, feature_table, token_table, tables, weights):
    plane, columns, length = blocks.shape
    rows = length // plane
    features = plane * columns
    w_query, w_key, w_value, w_out = weights
    sizes = (plane, columns, length, rows, w_query.shape[1] // HEAD, w_key.shape[1] // HEAD)
    vmem = pl.BlockSpec(memory_space=pltpu.VMEM)
    smem = pl.BlockSpec(memory_space=pltpu.SMEM)
    anywhere = pl.BlockSpec(memory_space=pl.ANY)
    width = w_query.shape[1] + w_key.shape[1] + w_value.shape[1]
    total = w_out.shape[1]
    return pl.pallas_call(
        lambda *refs: attention_body(sizes, *refs),
        out_shape=(
            jax.ShapeDtypeStruct((length // 2, total), F32),
            jax.ShapeDtypeStruct((length // 2, total), BF),
            jax.ShapeDtypeStruct((rows, features), F32),
        ),
        in_specs=[smem] * 2 + [vmem] * 6 + [anywhere] * 4,
        out_specs=(vmem,) * 3,
        scratch_shapes=[
            pltpu.VMEM((features, width), BF),
            pltpu.VMEM(w_out.shape, BF),
            pltpu.VMEM((features, length), BF),
            pltpu.VMEM((features, length), BF),
            pltpu.VMEM((length, w_query.shape[1]), F32),
            pltpu.SemaphoreType.DMA((4,)),
        ],
        compiler_params=pltpu.CompilerParams(vmem_limit_bytes=VMEM_LIMIT),
        cost_estimate=pl.CostEstimate(
            flops=2 * length * (features * width + w_query.shape[1] * total),
            bytes_accessed=2 * (features * width + w_out.size),
            transcendentals=0,
        ),
    )(
        feature_table,
        token_table,
        blocks,
        *tables,
        w_query,
        w_key,
        w_value,
        w_out,
    )


def local(
    residual,
    segments,
    row_perm,
    pre_gain,
    post_gain,
    w_query,
    w_key,
    w_value,
    w_out,
    sae_weight,
    enc_bias,
    thresholds,
    dec_bias,
):
    groups = lax.axis_size("dp")
    tensor, latent = lax.axis_size("tensor"), lax.axis_size("latent")
    plane = tensor * latent
    length = residual.shape[0]
    rows = length // plane
    half = sae_weight.shape[0]
    me = plane_index()
    mine = lax.axis_index("dp")
    cores = 2 if tensor % 2 == 0 else 1
    contract_last = (((1,), (1,)), ((), ()))

    tables = list(attention_tables(segments[0], pre_gain, me, rows))
    flat = jnp.arange(plane, dtype=jnp.int32)
    t_of, z_of = flat // latent, flat % latent
    number = ((t_of % cores) * (tensor // cores) + t_of // cores) * latent + z_of
    tables += [number ^ me, flat ^ me]

    def gate(pieces):
        held = lax.optimization_barrier(pieces + tables)
        tables[:] = held[len(pieces) :]
        return held[: len(pieces)]

    blocks = gather_blocks(residual.T[None], gate)
    kept_rows, sent_rows, own = attention(
        blocks, tables[-2], tables[-1], tables[:-2], (w_query, w_key, w_value, w_out)
    )
    attn_out = add_arrived(kept_rows, [sent_rows], plane_stages()[0])
    attn_out = scatter_sum(attn_out, 1)
    scale = lax.rsqrt(jnp.mean(attn_out * attn_out, axis=-1, keepdims=True) + epsilon)
    hidden = (own + attn_out * scale * post_gain).astype(BF)
    pieces = hidden.reshape(rows, groups, half).transpose(1, 0, 2)

    def piece(k):
        return lax.dynamic_index_in_dim(pieces, mine ^ k, 0, keepdims=False)

    others = jnp.stack([swap(piece(k), "dp", k) for k in range(1, groups)], 0)

    def spread(stack):
        count = stack.shape[0]
        if count == 1:
            return gather_blocks(stack[0])
        out = gather_blocks(stack.transpose(1, 0, 2).reshape(rows, count * half))
        out = out.reshape(length, count, half).transpose(1, 0, 2)
        return out.reshape(count * length, half)

    weights = {}

    def keep_weight(name):
        def gate(pieces):
            held = hold_on_chip(sae_weight, pieces[0])
            held = lax.optimization_barrier(pieces + [held])
            weights[name] = held[-1]
            return held[:-1]

        return gate

    sae = [gather_blocks(piece(0), keep_weight("pre_a")), spread(others)]

    def partial_pair(values, label):
        out = jnp.dot(values, weights.get(label, sae_weight), preferred_element_type=F32)
        return lax.optimization_barrier((out, out.astype(BF)))

    def across(chunks, label):
        (first_part, first_sent), (rest, rest_sent) = [
            partial_pair(c, f"{label}_{k}") for k, c in zip("ab", chunks)
        ]
        if groups == 2:
            got_rest = swap(first_sent, "dp", 1)
            got_first = swap(rest_sent, "dp", 1)
            return (first_part, got_first), (rest, got_rest)
        total = jnp.concatenate([first_part, rest], 0)
        masks = [1 << k for k in range(groups.bit_length() - 1)]
        for m in reversed(masks):
            keep, send = jnp.split(total, 2, axis=0)
            total = keep + swap(send.astype(BF), "dp", m).astype(F32)
        for m in masks:
            total = jnp.concatenate([total, swap(total, "dp", m)], 0)
        none = jnp.zeros((), BF)
        return (total[:length], none), (total[length:], none)

    def opened(own_part, arrived):
        pre = own_part + arrived.astype(F32) + enc_bias
        gate = jax.nn.sigmoid((pre - thresholds) / ramp_width)
        slope = gate + pre * gate * (1.0 - gate) / ramp_width
        return lax.optimization_barrier(((pre * gate).astype(BF), slope))

    codes, slopes = [None, None], [None, None]
    (first_part, first_arrived), (rest, rest_arrived) = across(sae, "pre")
    codes[1], slopes[1] = opened(rest, rest_arrived)
    _, first_arrived = lax.optimization_barrier((codes[1], first_arrived))
    codes[0], slopes[0] = opened(first_part, first_arrived)

    half_bias = lax.dynamic_slice(dec_bias, (mine * half,), (half,))

    def rebuild(chunk, count, after):
        part = lax.dot_general(codes[chunk], sae_weight, contract_last, preferred_element_type=F32)
        if count > 1:
            part = part.reshape(count, plane, rows, half).transpose(1, 0, 2, 3)
            part = part.reshape(plane * count * rows, half)
        total = scatter_sum(part)
        if count > 1:
            held = sae[chunk].reshape(count, plane, rows, half)[:, 0].reshape(count * rows, half)
        else:
            held = sae[chunk][:rows]
        if after is not None:
            total, _ = lax.optimization_barrier((total, after))
        error = (total + half_bias - held.astype(F32)).astype(BF)
        error = lax.optimization_barrier(error)
        out = gather_blocks(error, keep_weight("lat_b") if chunk else None)
        if count > 1:
            out = out.reshape(plane, count, rows, half).transpose(1, 0, 2, 3)
            out = out.reshape(count * length, half)
        return out, error

    error = [None, None]
    error[1], after = rebuild(1, groups - 1, None)
    error[0], _ = rebuild(0, 1, after)
    grad_scale = 1.0 / math.sqrt(length * groups)
    (first_part, first_arrived), (rest, rest_arrived) = across(error, "lat")
    grad_pre = [None, None]
    grad_pre[0] = ((first_part + first_arrived.astype(F32)) * slopes[0]).astype(BF)
    _, rest_arrived = lax.optimization_barrier((grad_pre[0], rest_arrived))
    grad_pre[1] = ((rest + rest_arrived.astype(F32)) * slopes[1]).astype(BF)
    total, hidden_t = early_gradient(error, codes, sae)
    weight_grad = late_gradient(total, hidden_t, grad_pre, grad_scale)
    bias_grad = grad_scale * sum(jnp.sum(g.astype(F32), axis=0) for g in grad_pre)

    place = row_perm ^ ((mine * plane + me) * rows)
    chosen = (place[:, None] == jnp.arange(length * groups, dtype=jnp.int32)[None, :]).astype(BF)
    out_codes = jnp.dot(chosen, jnp.concatenate(codes, 0), preferred_element_type=F32).astype(BF)
    return (weight_grad, bias_grad, out_codes)


def early_gradient(error, codes, hidden):
    tokens = sum(e.shape[0] for e in error)
    half, latents = error[0].shape[1], codes[0].shape[1]
    first = error[0].shape[0]

    def body(error_a, error_b, codes_a, codes_b, hidden_a, hidden_b, total, turned, left, right):
        left[:, :first] = error_a[...].T
        left[:, first:] = error_b[...].T
        right[:first] = codes_a[...]
        right[first:] = codes_b[...]
        total[...] = jnp.dot(left[...], right[...], preferred_element_type=F32)
        turned[:, :first] = hidden_a[...].T
        turned[:, first:] = hidden_b[...].T

    vmem = pl.BlockSpec(memory_space=pltpu.VMEM)
    return pl.pallas_call(
        body,
        out_shape=(pltpu.VMEM((half, latents), F32), pltpu.VMEM((half, tokens), BF)),
        in_specs=[vmem] * 6,
        out_specs=(vmem,) * 2,
        scratch_shapes=[pltpu.VMEM((half, tokens), BF), pltpu.VMEM((tokens, latents), BF)],
        compiler_params=pltpu.CompilerParams(vmem_limit_bytes=VMEM_LIMIT),
        cost_estimate=pl.CostEstimate(
            flops=2 * half * latents * tokens, bytes_accessed=4 * half * latents, transcendentals=0
        ),
    )(*error, *codes, *hidden)


def late_gradient(total, turned, grad_pre, grad_scale):
    half, latents = total.shape
    tile = max(t for t in range(16, 257, 16) if half % t == 0)
    first = grad_pre[0].shape[0]

    steps = half // tile

    def body(total, turned, grad_a, grad_b, out, right, ready, sems):
        right[:first] = grad_a[...]
        right[first:] = grad_b[...]

        def put(i):
            part = pl.ds(i * tile, tile)
            return pltpu.make_async_copy(ready.at[part], out.at[part], sems.at[i])

        for i in range(steps):
            part = pl.ds(i * tile, tile)
            product = jnp.dot(turned[part], right[...], preferred_element_type=F32)
            ready[part] = (grad_scale * (total[part] + product)).astype(BF)
            put(i).start()
        for i in range(steps):
            put(i).wait()

    vmem = pl.BlockSpec(memory_space=pltpu.VMEM)
    return pl.pallas_call(
        body,
        out_shape=jax.ShapeDtypeStruct((half, latents), BF),
        in_specs=[vmem] * 4,
        out_specs=pl.BlockSpec(memory_space=pltpu.HBM),
        scratch_shapes=[
            pltpu.VMEM((turned.shape[1], latents), BF),
            pltpu.VMEM((half, latents), BF),
            pltpu.SemaphoreType.DMA((steps,)),
        ],
        compiler_params=pltpu.CompilerParams(vmem_limit_bytes=VMEM_LIMIT),
        cost_estimate=pl.CostEstimate(
            flops=2 * half * latents * turned.shape[1],
            bytes_accessed=6 * half * latents,
            transcendentals=0,
        ),
    )(total, turned, *grad_pre)


def solution(mesh):
    return jax.shard_map(
        local,
        mesh=mesh,
        in_specs=(
            P("dp", ("tensor", "latent")),
            P("dp", None),
            P("dp"),
            P(),
            P(),
            P(None, ("tensor", "latent")),
            P(None, ("tensor", "latent")),
            P(None, ("tensor", "latent")),
            P(("tensor", "latent"), None),
            P("dp", ("tensor", "latent")),
            P(("tensor", "latent")),
            P(("tensor", "latent")),
            P(),
        ),
        out_specs=(
            P("dp", ("tensor", "latent")),
            P(("tensor", "latent")),
            P("dp", ("tensor", "latent")),
        ),
        check_vma=False,
    )
```

```python
import math

import jax
import jax.numpy as jnp
from jax import lax
from jax.experimental import pallas as pl
from jax.experimental.pallas import tpu as pltpu
from jax.sharding import PartitionSpec as P


D = 4608
HEADS = 32
HEAD = 128

epsilon = 1e-06
softcap = 50.0
ramp_width = 0.05
rotary_base = 10000.0
BF = jnp.bfloat16
F32 = jnp.float32
VMEM_LIMIT = 28 * 1024 * 1024


def swap(values, axis, mask):
    size = lax.axis_size(axis)
    return lax.ppermute(values, axis, [(i, i ^ mask) for i in range(size)])


def plane_stages():
    tensor, latent = lax.axis_size("tensor"), lax.axis_size("latent")
    cores = 2 if tensor % 2 == 0 else 1
    stages = []
    if cores > 1:
        stages.append(("tensor", [1]))
    if tensor > cores:
        stages.append(("tensor", [k * cores for k in range(1, tensor // cores)]))
    if latent > 1:
        stages.append(("latent", list(range(1, latent))))
    return stages


def plane_index():
    tensor, latent = lax.axis_size("tensor"), lax.axis_size("latent")
    cores = 2 if tensor % 2 == 0 else 1
    t, z = lax.axis_index("tensor"), lax.axis_index("latent")
    return ((t % cores) * (tensor // cores) + t // cores) * latent + z


def gather_blocks(block, gate=None):
    stages = plane_stages()
    for place in reversed(range(len(stages))):
        axis, masks = stages[place]
        pieces = [block] + [swap(block, axis, m) for m in masks]
        if place == 1 and gate is not None:
            pieces = gate(pieces)
        block = jnp.concatenate(pieces, axis=0)
    return block


def add_arrived(kept, sent, stage):
    axis, masks = stage
    arrived = [swap(part, axis, m) for m, part in zip(masks, sent)]
    total = kept
    for part in arrived:
        total = total + part.astype(F32)
    return total


def scatter_sum(partial, done=0):
    for place, stage in enumerate(plane_stages()):
        if place < done:
            continue
        parts = partial.reshape((len(stage[1]) + 1, -1) + partial.shape[1:])
        sent = [parts[k + 1].astype(BF) for k in range(len(stage[1]))]
        partial = add_arrived(parts[0].astype(F32), sent, stage)
    return partial


def rotary_tables(positions):
    half_width = HEAD // 2
    frequency = rotary_base ** (-2.0 * jnp.arange(half_width, dtype=F32) / HEAD)
    angles = positions[:, None] * frequency
    cosine, sine = jnp.cos(angles), jnp.sin(angles)
    return jnp.concatenate([cosine, cosine], 1), jnp.concatenate([-sine, sine], 1)


def doc_masks(segment_ids):
    same_doc = segment_ids[..., :, None] == segment_ids[..., None, :]
    indices = jnp.arange(segment_ids.shape[-1], dtype=jnp.int32)
    earlier = indices[None, :] < indices[:, None]
    positions = jnp.sum((same_doc & earlier).astype(F32), axis=-1)
    attend_mask = (same_doc & (indices[None, :] <= indices[:, None])).astype(F32)
    return (positions, attend_mask)


def hold_on_chip(values, after):
    def body(source, _, held, sem):
        copy = pltpu.make_async_copy(source, held, sem)
        copy.start()
        copy.wait()

    return pl.pallas_call(
        body,
        out_shape=pltpu.VMEM(values.shape, values.dtype),
        in_specs=[pl.BlockSpec(memory_space=pltpu.HBM), pl.BlockSpec(memory_space=pl.ANY)],
        out_specs=pl.BlockSpec(memory_space=pltpu.VMEM),
        scratch_shapes=[pltpu.SemaphoreType.DMA],
        compiler_params=pltpu.CompilerParams(vmem_limit_bytes=1024 * 1024),
        cost_estimate=pl.CostEstimate(
            flops=0, bytes_accessed=2 * values.size, transcendentals=0
        ),
    )(values, after)


def attention_body(
    sizes,
    feature_table,
    token_table,
    blocks,
    gain,
    cosine,
    sine,
    mask,
    pick,
    w_query,
    w_key,
    w_value,
    w_out,
    kept,
    sent,
    own,
    weight,
    weight_out,
    stream,
    normed,
    heads,
    sems,
):
    plane, columns, length, rows, query_heads, key_heads = sizes
    query_width, key_width = query_heads * HEAD, key_heads * HEAD
    starts = [0, query_width, query_width + key_width]
    copies = [
        pltpu.make_async_copy(src, weight.at[:, pl.ds(start, src.shape[1])], sems.at[k])
        for k, (src, start) in enumerate(zip((w_query, w_key, w_value), starts))
    ]
    copies.append(pltpu.make_async_copy(w_out, weight_out, sems.at[3]))
    for copy in copies:
        copy.start()
    squares = jnp.zeros((1, length), F32)
    for j in range(plane):
        block = blocks[feature_table[j]]
        stream[j * columns : (j + 1) * columns] = block
        wide = block.astype(F32)
        squares = squares + jnp.sum(wide * wide, axis=0, keepdims=True)
    scale = lax.rsqrt(squares / (plane * columns) + epsilon)
    for j in range(plane):
        part = slice(j * columns, (j + 1) * columns)
        normed[part] = (stream[part].astype(F32) * scale * gain[part]).astype(BF)
    own[...] = lax.dot_general(
        pick[...], stream[...], (((1,), (1,)), ((), ())), preferred_element_type=F32
    )
    for copy in copies[:3]:
        copy.wait()
    projected = lax.dot_general(
        normed[...], weight[...], (((0,), (0,)), ((), ())), preferred_element_type=F32
    )

    def turned(start):
        field = projected[:, start : start + HEAD]
        return (field * cosine[...] + pltpu.roll(field, HEAD // 2, 1) * sine[...]).astype(BF)

    for j in range(query_heads):
        group = j // (query_heads // key_heads)
        query = turned(j * HEAD)
        key = turned(starts[1] + group * HEAD)
        value = projected[:, starts[2] + group * HEAD : starts[2] + (group + 1) * HEAD].astype(BF)
        logits = lax.dot_general(
            query, key, (((1,), (1,)), ((), ())), preferred_element_type=F32
        ) * (D / HEADS) ** (-0.5)
        logits = softcap * jnp.tanh(logits / softcap)
        weighted = jnp.exp(logits) * mask[...]
        probs = (weighted / jnp.sum(weighted, axis=-1, keepdims=True)).astype(BF)
        heads[:, j * HEAD : (j + 1) * HEAD] = jnp.dot(probs, value, preferred_element_type=F32)
    moved = [heads[pl.ds(pl.multiple_of(token_table[k] * rows, 8), rows)] for k in range(plane)]
    moved = jnp.concatenate(moved, 0).astype(BF)
    copies[3].wait()
    middle = length // 2
    step = 512
    for start in range(0, weight_out.shape[1], step):
        part = slice(start, min(start + step, weight_out.shape[1]))
        product = jnp.dot(moved, weight_out[:, part], preferred_element_type=F32)
        kept[:, part] = product[:middle]
        sent[:, part] = product[middle:].astype(BF)


def attention_tables(segments, pre_gain, me, rows):
    length = segments.shape[0]
    positions, mask = doc_masks(segments)
    cosine, sine = rotary_tables(positions)
    gain = jnp.broadcast_to(pre_gain[:, None], (pre_gain.shape[0], length))
    token = jnp.arange(length, dtype=jnp.int32)[None, :]
    pick = (token == me * rows + jnp.arange(rows, dtype=jnp.int32)[:, None]).astype(BF)
    return gain, cosine, sine, mask, pick


def attention(blocks, feature_table, token_table, tables, weights):
    plane, columns, length = blocks.shape
    rows = length // plane
    features = plane * columns
    w_query, w_key, w_value, w_out = weights
    sizes = (plane, columns, length, rows, w_query.shape[1] // HEAD, w_key.shape[1] // HEAD)
    vmem = pl.BlockSpec(memory_space=pltpu.VMEM)
    smem = pl.BlockSpec(memory_space=pltpu.SMEM)
    anywhere = pl.BlockSpec(memory_space=pl.ANY)
    width = w_query.shape[1] + w_key.shape[1] + w_value.shape[1]
    total = w_out.shape[1]
    return pl.pallas_call(
        lambda *refs: attention_body(sizes, *refs),
        out_shape=(
            jax.ShapeDtypeStruct((length // 2, total), F32),
            jax.ShapeDtypeStruct((length // 2, total), BF),
            jax.ShapeDtypeStruct((rows, features), F32),
        ),
        in_specs=[smem] * 2 + [vmem] * 6 + [anywhere] * 4,
        out_specs=(vmem,) * 3,
        scratch_shapes=[
            pltpu.VMEM((features, width), BF),
            pltpu.VMEM(w_out.shape, BF),
            pltpu.VMEM((features, length), BF),
            pltpu.VMEM((features, length), BF),
            pltpu.VMEM((length, w_query.shape[1]), F32),
            pltpu.SemaphoreType.DMA((4,)),
        ],
        compiler_params=pltpu.CompilerParams(vmem_limit_bytes=VMEM_LIMIT),
        cost_estimate=pl.CostEstimate(
            flops=2 * length * (features * width + w_query.shape[1] * total),
            bytes_accessed=2 * (features * width + w_out.size),
            transcendentals=0,
        ),
    )(
        feature_table,
        token_table,
        blocks,
        *tables,
        w_query,
        w_key,
        w_value,
        w_out,
    )


def local(
    residual,
    segments,
    row_perm,
    pre_gain,
    post_gain,
    w_query,
    w_key,
    w_value,
    w_out,
    sae_weight,
    enc_bias,
    thresholds,
    dec_bias,
):
    groups = lax.axis_size("dp")
    tensor, latent = lax.axis_size("tensor"), lax.axis_size("latent")
    plane = tensor * latent
    length = residual.shape[0]
    rows = length // plane
    half = sae_weight.shape[0]
    me = plane_index()
    mine = lax.axis_index("dp")
    cores = 2 if tensor % 2 == 0 else 1
    contract_last = (((1,), (1,)), ((), ()))

    tables = list(attention_tables(segments[0], pre_gain, me, rows))
    flat = jnp.arange(plane, dtype=jnp.int32)
    t_of, z_of = flat // latent, flat % latent
    number = ((t_of % cores) * (tensor // cores) + t_of // cores) * latent + z_of
    tables += [number ^ me, flat ^ me]
    place = row_perm ^ ((mine * plane + me) * rows)
    chosen = (place[:, None] == jnp.arange(length * groups, dtype=jnp.int32)[None, :]).astype(BF)
    starts = [(mine ^ k) * half for k in range(groups)]
    half_bias = lax.dynamic_slice(dec_bias, (starts[0],), (half,), allow_negative_indices=False)
    tables += [chosen, half_bias] + starts

    def gate(pieces):
        held = lax.optimization_barrier(pieces + tables)
        tables[:] = held[len(pieces) :]
        return held[: len(pieces)]

    blocks = gather_blocks(residual.T[None], gate)
    kept_rows, sent_rows, own = attention(
        blocks, tables[5], tables[6], tables[:5], (w_query, w_key, w_value, w_out)
    )
    chosen, half_bias, *starts = tables[7:]
    attn_out = add_arrived(kept_rows, [sent_rows], plane_stages()[0])
    attn_out = scatter_sum(attn_out, 1)
    scale = lax.rsqrt(jnp.mean(attn_out * attn_out, axis=-1, keepdims=True) + epsilon)
    hidden = (own + attn_out * scale * post_gain).astype(BF)

    def piece(k):
        return lax.dynamic_slice(
            hidden, (0, starts[k]), (rows, half), allow_negative_indices=False
        )

    others = jnp.stack([swap(piece(k), "dp", k) for k in range(1, groups)], 0)

    def spread(stack):
        count = stack.shape[0]
        if count == 1:
            return gather_blocks(stack[0])
        out = gather_blocks(stack.transpose(1, 0, 2).reshape(rows, count * half))
        out = out.reshape(length, count, half).transpose(1, 0, 2)
        return out.reshape(count * length, half)

    weights = {}

    def keep_weight(name):
        def gate(pieces):
            held = hold_on_chip(sae_weight, pieces[0])
            held = lax.optimization_barrier(pieces + [held])
            weights[name] = held[-1]
            return held[:-1]

        return gate

    sae = [gather_blocks(piece(0), keep_weight("pre_a")), spread(others)]

    def partial_pair(values, label):
        out = jnp.dot(values, weights.get(label, sae_weight), preferred_element_type=F32)
        return lax.optimization_barrier((out, out.astype(BF)))

    def across(chunks, label):
        (first_part, first_sent), (rest, rest_sent) = [
            partial_pair(c, f"{label}_{k}") for k, c in zip("ab", chunks)
        ]
        if groups == 2:
            got_rest = swap(first_sent, "dp", 1)
            got_first = swap(rest_sent, "dp", 1)
            return (first_part, got_first), (rest, got_rest)
        total = jnp.concatenate([first_part, rest], 0)
        masks = [1 << k for k in range(groups.bit_length() - 1)]
        for m in reversed(masks):
            keep, send = jnp.split(total, 2, axis=0)
            total = keep + swap(send.astype(BF), "dp", m).astype(F32)
        for m in masks:
            total = jnp.concatenate([total, swap(total, "dp", m)], 0)
        none = jnp.zeros((), BF)
        return (total[:length], none), (total[length:], none)

    def opened(own_part, arrived):
        pre = own_part + arrived.astype(F32) + enc_bias
        gate = jax.nn.sigmoid((pre - thresholds) / ramp_width)
        slope = gate + pre * gate * (1.0 - gate) / ramp_width
        return lax.optimization_barrier(((pre * gate).astype(BF), slope))

    codes, slopes = [None, None], [None, None]
    (first_part, first_arrived), (rest, rest_arrived) = across(sae, "pre")
    codes[1], slopes[1] = opened(rest, rest_arrived)
    _, first_arrived = lax.optimization_barrier((codes[1], first_arrived))
    codes[0], slopes[0] = opened(first_part, first_arrived)

    def rebuild(chunk, count, after):
        if count == 1:
            kept, sent = rebuild_split(codes[chunk], sae_weight)
            total = add_arrived(kept, [sent], plane_stages()[0])
            total = scatter_sum(total, 1)
        else:
            part = lax.dot_general(
                codes[chunk], sae_weight, contract_last, preferred_element_type=F32
            )
            part = part.reshape(count, plane, rows, half).transpose(1, 0, 2, 3)
            total = scatter_sum(part.reshape(plane * count * rows, half))
        if count > 1:
            held = sae[chunk].reshape(count, plane, rows, half)[:, 0].reshape(count * rows, half)
        else:
            held = sae[chunk][:rows]
        if after is not None:
            total, _ = lax.optimization_barrier((total, after))
        error = (total + half_bias - held.astype(F32)).astype(BF)
        error = lax.optimization_barrier(error)
        out = gather_blocks(error, keep_weight("lat_b") if chunk else None)
        if count > 1:
            out = out.reshape(plane, count, rows, half).transpose(1, 0, 2, 3)
            out = out.reshape(count * length, half)
        return out, error

    error = [None, None]
    error[1], after = rebuild(1, groups - 1, None)
    error[0], _ = rebuild(0, 1, after)
    grad_scale = 1.0 / math.sqrt(length * groups)
    (first_part, first_arrived), (rest, rest_arrived) = across(error, "lat")
    grad_pre = [None, None]
    grad_pre[0] = ((first_part + first_arrived.astype(F32)) * slopes[0]).astype(BF)
    _, rest_arrived = lax.optimization_barrier((grad_pre[0], rest_arrived))
    grad_pre[1] = ((rest + rest_arrived.astype(F32)) * slopes[1]).astype(BF)
    total, hidden_t = early_gradient(error, codes, sae)
    weight_grad, bias_grad = late_gradient(total, hidden_t, grad_pre, grad_scale)
    out_codes = jnp.dot(chosen, jnp.concatenate(codes, 0), preferred_element_type=F32).astype(BF)
    return (weight_grad, bias_grad.reshape(-1), out_codes)


def rebuild_split(codes, weight):
    count, half = codes.shape[0], weight.shape[0]
    middle = count // 2

    def body(codes, weight, kept, sent):
        product = lax.dot_general(
            codes[...], weight[...], (((1,), (1,)), ((), ())), preferred_element_type=F32
        )
        kept[...] = product[:middle]
        sent[...] = product[middle:].astype(BF)

    vmem = pl.BlockSpec(memory_space=pltpu.VMEM)
    return pl.pallas_call(
        body,
        out_shape=(
            jax.ShapeDtypeStruct((middle, half), F32),
            jax.ShapeDtypeStruct((count - middle, half), BF),
        ),
        in_specs=[vmem] * 2,
        out_specs=(vmem,) * 2,
        compiler_params=pltpu.CompilerParams(vmem_limit_bytes=16 * 1024 * 1024),
        cost_estimate=pl.CostEstimate(
            flops=2 * count * weight.size, bytes_accessed=2 * weight.size, transcendentals=0
        ),
    )(codes, weight)


def early_gradient(error, codes, hidden):
    tokens = sum(e.shape[0] for e in error)
    half, latents = error[0].shape[1], codes[0].shape[1]
    first = error[0].shape[0]

    def body(error_a, error_b, codes_a, codes_b, hidden_a, hidden_b, total, turned, left, right):
        left[:, :first] = error_a[...].T
        left[:, first:] = error_b[...].T
        right[:first] = codes_a[...]
        right[first:] = codes_b[...]
        total[...] = jnp.dot(left[...], right[...], preferred_element_type=F32)
        turned[:, :first] = hidden_a[...].T
        turned[:, first:] = hidden_b[...].T

    vmem = pl.BlockSpec(memory_space=pltpu.VMEM)
    return pl.pallas_call(
        body,
        out_shape=(pltpu.VMEM((half, latents), F32), pltpu.VMEM((half, tokens), BF)),
        in_specs=[vmem] * 6,
        out_specs=(vmem,) * 2,
        scratch_shapes=[pltpu.VMEM((half, tokens), BF), pltpu.VMEM((tokens, latents), BF)],
        compiler_params=pltpu.CompilerParams(vmem_limit_bytes=VMEM_LIMIT),
        cost_estimate=pl.CostEstimate(
            flops=2 * half * latents * tokens, bytes_accessed=4 * half * latents, transcendentals=0
        ),
    )(*error, *codes, *hidden)


def late_gradient(total, turned, grad_pre, grad_scale):
    half, latents = total.shape
    tile = max(t for t in range(16, 257, 16) if half % t == 0)
    first = grad_pre[0].shape[0]

    steps = half // tile

    def body(total, turned, grad_a, grad_b, out, bias, right, ready, sems):
        right[:first] = grad_a[...]
        right[first:] = grad_b[...]

        def put(i):
            part = pl.ds(i * tile, tile)
            return pltpu.make_async_copy(ready.at[part], out.at[part], sems.at[i])

        for i in range(steps):
            part = pl.ds(i * tile, tile)
            product = jnp.dot(turned[part], right[...], preferred_element_type=F32)
            ready[part] = (grad_scale * (total[part] + product)).astype(BF)
            put(i).start()
        bias[...] = grad_scale * (
            jnp.sum(grad_a[...].astype(F32), axis=0, keepdims=True)
            + jnp.sum(grad_b[...].astype(F32), axis=0, keepdims=True)
        )
        for i in range(steps):
            put(i).wait()

    vmem = pl.BlockSpec(memory_space=pltpu.VMEM)
    return pl.pallas_call(
        body,
        out_shape=(
            jax.ShapeDtypeStruct((half, latents), BF),
            jax.ShapeDtypeStruct((1, latents), F32),
        ),
        in_specs=[vmem] * 4,
        out_specs=(pl.BlockSpec(memory_space=pltpu.HBM), vmem),
        scratch_shapes=[
            pltpu.VMEM((turned.shape[1], latents), BF),
            pltpu.VMEM((half, latents), BF),
            pltpu.SemaphoreType.DMA((steps,)),
        ],
        compiler_params=pltpu.CompilerParams(vmem_limit_bytes=VMEM_LIMIT),
        cost_estimate=pl.CostEstimate(
            flops=2 * half * latents * turned.shape[1],
            bytes_accessed=6 * half * latents,
            transcendentals=0,
        ),
    )(total, turned, *grad_pre)


def solution(mesh):
    return jax.shard_map(
        local,
        mesh=mesh,
        in_specs=(
            P("dp", ("tensor", "latent")),
            P("dp", None),
            P("dp"),
            P(),
            P(),
            P(None, ("tensor", "latent")),
            P(None, ("tensor", "latent")),
            P(None, ("tensor", "latent")),
            P(("tensor", "latent"), None),
            P("dp", ("tensor", "latent")),
            P(("tensor", "latent")),
            P(("tensor", "latent")),
            P(),
        ),
        out_specs=(
            P("dp", ("tensor", "latent")),
            P(("tensor", "latent")),
            P("dp", ("tensor", "latent")),
        ),
        check_vma=False,
    )
```
